32 devices in a mesh: ctx: 16 (over z, x, core), head: 2 (over y).
Axes of the slice: x: 2, y: 2, z: 4, core: 2. Of those that a mesh axis runs over, the one named last changes fastest.
Arguments:
- queries: bfloat16 [4096, 8192], P(('ctx', 'head')), may hold values from -6 to 6
- key_heads: bfloat16 [4096, 1024], P(('ctx', 'head')), may hold values from -6 to 6
- value_head_array: bfloat16 [4096, 1024], P(('ctx', 'head')), may hold values from -6 to 6
- out_grad: bfloat16 [4096, 8192], P(('ctx', 'head')), may hold values from -6 to 6
- doc_ids: int32 [4096], P('ctx'), may hold values from 0 to 63, never falling along the last dimension, each value on 1 to 1792 neighbouring positions
Outputs:
- attended: bfloat16 [4096, 8192], P(('ctx', 'head'))
- query_grad: bfloat16 [4096, 8192], P(('ctx', 'head'))
- key_grad: bfloat16 [4096, 1024], P(('ctx', 'head'))
- value_grad: bfloat16 [4096, 1024], P(('ctx', 'head'))
The draws below stay inside these ranges and needn't reach their ends.
Inputs may be any that keep to these rules, and one draw needn't show every extreme that they name: `doc_ids`: document numbers never fall along the batch; each document holds 1 to 1792 consecutive tokens and one holds exactly 1792.
All inputs are finite; a program needn't handle non-finite values.
Results may differ from the reference program's by a relative error of at most 0.022.
Values may be sent and summed in bfloat16 or wider, within the bound.
A program may use at most 192 MiB of HBM per device.

```python
import math
import jax
import jax.numpy as jnp
import numpy as np
from jax import lax

QUERY_HEADS = 64
KEY_VALUE_HEADS = 8
HEAD_SIZE = 128
WINDOW = 1536
PACKED_TOKENS = 4096
DOCS = 64
DOC_MOST = 1792


def paired_fields(key):
    folded = jax.random.fold_in(key, 11)
    random_subkeys = jax.random.split(folded, 2)
    query_all = jnp.clip(jax.random.normal(random_subkeys[0], (PACKED_TOKENS, QUERY_HEADS * HEAD_SIZE), jnp.float32), -6.0, 6.0)
    every_key = jnp.clip(jax.random.normal(random_subkeys[1], (PACKED_TOKENS, KEY_VALUE_HEADS * HEAD_SIZE), jnp.float32), -6.0, 6.0)
    return (query_all, every_key)


def draw_queries(key, part):
    return paired_fields(key)[0].astype(jnp.bfloat16)


def draw_key_heads(key, part):
    return paired_fields(key)[1].astype(jnp.bfloat16)


def block_scale(stream_key, shape, shards, low, high):
    def one(position, blocks):
        steps = jax.random.uniform(jax.random.fold_in(jax.random.fold_in(stream_key, 6), position), (blocks,), jnp.float32, low / len(shards), high / len(shards))
        return jnp.repeat(jnp.exp(steps), shape[position] // blocks).reshape((-1,) + (1,) * (len(shape) - position - 1))

    factor_of = one(*shards[0])
    for cut in shards[1:]:
        factor_of = factor_of * one(*cut)
    return factor_of


def length_profile(number_of, total, limit, lean):
    weights = [(1 << 20) // math.isqrt(grade ** lean) + 1 for grade in range(2, number_of + 1)]
    spare, holding = total - limit - (number_of - 1), [1] * (number_of - 1)
    while spare > 0:
        candidates = [i for i in range(number_of - 1) if holding[i] < limit]
        pool, left = sum([weights[i] for i in candidates]), spare
        for i in candidates:
            more = min(limit - holding[i], max(1, left * weights[i] // pool), spare)
            holding[i] = holding[i] + more
            spare = spare - more
    return np.array([limit] + holding)


def uneven_parts(key, amount, total, bound, slope):
    if amount == 2:
        one = jax.random.randint(key, (), max(1, total - bound), min(bound, total - 1) + 1)
        return jnp.stack([one, total - one])
    sizes = jnp.asarray(length_profile(amount, total, bound, slope), jnp.int32)
    pairs = (amount - 1) // 2
    giver, sink = sizes[1:1 + 2 * pairs:2], sizes[2:2 + 2 * pairs:2]
    room = jnp.minimum(giver - 1, bound - sink)
    shifted = jax.random.randint(jax.random.fold_in(key, 1), (pairs,), 0, 1 << 20) % (room + 1)
    sizes = sizes.at[1:1 + 2 * pairs:2].set(giver - shifted).at[2:2 + 2 * pairs:2].set(sink + shifted)
    return sizes[jax.random.permutation(jax.random.fold_in(key, 2), amount)]


def scatter_about(own_key, dims, deviation, limit, shards=(), kind=jnp.bfloat16):
    result = deviation * jax.random.normal(own_key, dims, jnp.float32)
    if shards:
        result = result * block_scale(own_key, dims, shards, -0.22, 0.18)
    return jnp.clip(result, -limit, limit).astype(kind)


def setup_inputs(seed: int = 0) -> dict:
    arg_keys = jax.random.split(jax.random.key(seed), 6)
    return {
        "queries": draw_queries(jax.random.fold_in(arg_keys[5], 71), 0),
        "key_heads": draw_key_heads(jax.random.fold_in(arg_keys[5], 71), 0),
        "value_head_array": scatter_about(arg_keys[2], (PACKED_TOKENS, KEY_VALUE_HEADS * HEAD_SIZE), 1.0, 6.0, ((0, 32),)),
        "out_grad": scatter_about(arg_keys[3], (PACKED_TOKENS, QUERY_HEADS * HEAD_SIZE), 1.0, 6.0, ((0, 32),)),
        "doc_ids": jnp.searchsorted(jnp.cumsum(uneven_parts(arg_keys[4], DOCS, PACKED_TOKENS, DOC_MOST, 2)), jnp.arange(PACKED_TOKENS), side="right").astype(jnp.int32),
    }


def reference(queries, key_heads, value_head_array, out_grad, doc_ids):
    total_rows = queries.shape[0]
    kv_width = key_heads.shape[1]
    kv_heads = kv_width // HEAD_SIZE
    group_size = queries.shape[1] // kv_width
    block_rows = math.gcd(total_rows, 128)
    key_span = block_rows + WINDOW
    score_scale = HEAD_SIZE ** -0.5
    key_pad = jnp.concatenate([jnp.zeros((WINDOW, kv_width), key_heads.dtype), key_heads], axis=0)
    value_pad = jnp.concatenate([jnp.zeros((WINDOW, kv_width), value_head_array.dtype), value_head_array], axis=0)
    doc_pad = jnp.concatenate([jnp.full((WINDOW,), -1, jnp.int32), doc_ids.astype(jnp.int32)])

    def step(carry, block_index):
        key_acc, value_acc = carry
        first_row = (block_index * block_rows).astype(jnp.int32)
        query_four = lax.dynamic_slice_in_dim(queries, first_row, block_rows, 0).astype(jnp.float32).reshape(block_rows, kv_heads, group_size, HEAD_SIZE)
        grad_four = lax.dynamic_slice_in_dim(out_grad, first_row, block_rows, 0).astype(jnp.float32).reshape(block_rows, kv_heads, group_size, HEAD_SIZE)
        key_three = lax.dynamic_slice_in_dim(key_pad, first_row, key_span, 0).astype(jnp.float32).reshape(key_span, kv_heads, HEAD_SIZE)
        value_three = lax.dynamic_slice_in_dim(value_pad, first_row, key_span, 0).astype(jnp.float32).reshape(key_span, kv_heads, HEAD_SIZE)
        query_pos = first_row + jnp.arange(block_rows, dtype=jnp.int32)
        key_pos = first_row - WINDOW + jnp.arange(key_span, dtype=jnp.int32)
        query_doc = lax.dynamic_slice_in_dim(doc_ids.astype(jnp.int32), first_row, block_rows, 0)
        key_doc = lax.dynamic_slice_in_dim(doc_pad, first_row, key_span, 0)
        distance = query_pos[:, None] - key_pos[None, :]
        visible = (query_doc[:, None] == key_doc[None, :]) & (key_pos[None, :] >= 0) & (distance >= 0) & (distance < WINDOW)
        scores = jnp.einsum("qgpd,kgd->gpqk", query_four, key_three) * score_scale
        masked = jnp.where(visible, scores, -jnp.inf)
        row_max = jnp.max(masked, axis=-1, keepdims=True)
        log_total = row_max + jnp.log(jnp.sum(jnp.where(visible, jnp.exp(masked - row_max), 0.0), axis=-1, keepdims=True))
        prob_block = jnp.where(visible, jnp.exp(scores - log_total), 0.0)
        weights = prob_block.astype(jnp.bfloat16).astype(jnp.float32)
        out_rounded = jnp.einsum("gpqk,kgd->qgpd", weights, value_three).astype(jnp.bfloat16)
        row_delta = jnp.einsum("qgpd,qgpd->gpq", grad_four, out_rounded.astype(jnp.float32))[..., None]
        prob_grad = jnp.einsum("qgpd,kgd->gpqk", grad_four, value_three)
        score_grad = (prob_block * (prob_grad - row_delta)).astype(jnp.bfloat16).astype(jnp.float32)
        query_rows = (score_scale * jnp.einsum("gpqk,kgd->qgpd", score_grad, key_three)).astype(jnp.bfloat16)
        key_term = score_scale * jnp.einsum("gpqk,qgpd->kgd", score_grad, query_four)
        value_term = jnp.einsum("gpqk,qgpd->kgd", weights, grad_four)
        key_old = lax.dynamic_slice_in_dim(key_acc, first_row, key_span, 0)
        value_old = lax.dynamic_slice_in_dim(value_acc, first_row, key_span, 0)
        key_acc = lax.dynamic_update_slice_in_dim(key_acc, key_old + key_term.reshape(key_span, kv_width), first_row, 0)
        value_acc = lax.dynamic_update_slice_in_dim(value_acc, value_old + value_term.reshape(key_span, kv_width), first_row, 0)
        return (key_acc, value_acc), (out_rounded.reshape(block_rows, -1), query_rows.reshape(block_rows, -1))

    empty_acc = jnp.zeros((total_rows + WINDOW, kv_width), jnp.float32)
    (key_acc, value_acc), (out_blocks, query_blocks) = lax.scan(step, (empty_acc, empty_acc), jnp.arange(total_rows // block_rows, dtype=jnp.int32))
    attended = out_blocks.reshape(total_rows, -1)
    query_grad = query_blocks.reshape(total_rows, -1)
    key_grad = key_acc[WINDOW:].astype(jnp.bfloat16)
    value_grad = value_acc[WINDOW:].astype(jnp.bfloat16)
    return (attended, query_grad, key_grad, value_grad)
```

```python
import functools
import math

import jax
import jax.numpy as jnp
from jax import lax
from jax.experimental import pallas as pl
from jax.experimental.pallas import tpu as pltpu
from jax.sharding import PartitionSpec as P

HEAD_SIZE = 128
WINDOW = 1536
MASKED = -1e30
MESH = pl.DeviceIdType.MESH
VMEM = pl.BlockSpec(memory_space=pltpu.VMEM)


def remote(src, dst, send_sem, recv_sem, ctx, head):
    return pltpu.make_async_remote_copy(
        src_ref=src,
        dst_ref=dst,
        send_sem=send_sem,
        recv_sem=recv_sem,
        device_id={"ctx": ctx, "head": head},
        device_id_type=MESH,
    )


def greet(pairs, heads, back):
    ctx, head = lax.axis_index("ctx"), lax.axis_index("head")
    pair, core = ctx // 2, ctx % 2
    barrier = pltpu.get_barrier_semaphore()

    def signal(to_ctx, to_head):
        pl.semaphore_signal(
            barrier, inc=1, device_id={"ctx": to_ctx, "head": to_head}, device_id_type=MESH
        )

    signal(pair * 2 + 1 - core, head)
    for d in range(1, heads):
        signal(ctx, lax.rem(head + d, heads))
    for k in range(1, back + 1):
        for other in (pair + k, pair + pairs - k):
            signal(lax.rem(other, pairs) * 2 + core, head)
    pl.semaphore_wait(barrier, heads + 2 * back)


def gather_kernel(
    pairs, heads, back,
    q_ref, g_ref, kv_ref, doc_ref,
    q2, g2, win, docs,
    local_sem, core_send, core_recv, far_send, far_recv, head_send, head_recv, doc_send, doc_recv,
):
    ctx, head = lax.axis_index("ctx"), lax.axis_index("head")
    pair, core = ctx // 2, ctx % 2
    rows = q_ref.shape[0]
    half = q_ref.shape[1] // 2
    partner = pair * 2 + 1 - core
    mine = pl.ds(pl.multiple_of(head * rows, rows), rows)
    keep = pl.ds(pl.multiple_of(core * half, half), half)
    give = pl.ds(pl.multiple_of((1 - core) * half, half), half)

    def region(k, where=mine):
        return win.at[:, :, back - k, :, where, :]

    greet(pairs, heads, back)
    to_core = [
        remote(kv_ref.at[1 - core], win.at[:, :, back, core, mine, :], core_send.at[0], core_recv.at[0], partner, head),
        remote(doc_ref, docs.at[back, core], core_send.at[1], core_recv.at[1], partner, head),
        remote(q_ref.at[:, give], q2.at[core], core_send.at[2], core_recv.at[2], partner, head),
        remote(g_ref.at[:, give], g2.at[core], core_send.at[3], core_recv.at[3], partner, head),
    ]
    on_chip = [
        pltpu.make_async_copy(kv_ref.at[core], win.at[:, :, back, core, mine, :], local_sem.at[0]),
        pltpu.make_async_copy(doc_ref, docs.at[back, core], local_sem.at[1]),
        pltpu.make_async_copy(q_ref.at[:, keep], q2.at[core], local_sem.at[2]),
        pltpu.make_async_copy(g_ref.at[:, keep], g2.at[core], local_sem.at[3]),
    ]
    for copy in to_core + on_chip:
        copy.start()
    for k in range(1, back + 1):

        @pl.when(pair - k < 0)
        def _():
            win[:, :, back - k] = jnp.zeros(win.shape[:2] + win.shape[3:], win.dtype)
            docs[back - k] = jnp.full(docs.shape[1:], -1, docs.dtype)

    for n in range(2):
        on_chip[n].wait()
        to_core[n].wait_recv()

    def spread(k, d):
        return remote(
            region(k), region(k), head_send.at[d - 1, k], head_recv.at[d - 1, k],
            ctx, lax.rem(head + d, heads),
        )

    def ahead(k):
        to = ctx + 2 * k
        return (
            remote(region(0), region(k), far_send.at[k - 1], far_recv.at[k - 1], to, head),
            remote(docs.at[back], docs.at[back - k], doc_send.at[k - 1], doc_recv.at[k - 1], to, head),
        )

    for k in range(1, back + 1):

        @pl.when(pair + k < pairs)
        def _():
            for copy in ahead(k):
                copy.start()

    for d in range(1, heads):
        spread(0, d).start()
    for k in range(1, back + 1):

        @pl.when(pair - k >= 0)
        def _():
            for copy in ahead(k):
                copy.wait_recv()
            for d in range(1, heads):
                spread(k, d).start()

    for n in range(2, 4):
        on_chip[n].wait()
        to_core[n].wait_recv()
    for d in range(1, heads):
        spread(0, d).wait()
    for k in range(1, back + 1):

        @pl.when(pair - k >= 0)
        def _():
            for d in range(1, heads):
                spread(k, d).wait()

        @pl.when(pair + k < pairs)
        def _():
            for copy in ahead(k):
                copy.wait_send()

    for copy in to_core:
        copy.wait_send()


def attend_kernel(rows, heads_at_once, low_ref, q2, g2, win, out2, dq2, dkv, bias, acc):
    kv_heads, span = win.shape[1], win.shape[2]
    slots = q2.shape[0]
    group = q2.shape[2] // HEAD_SIZE // kv_heads
    block = (span - WINDOW) // slots
    length = WINDOW + rows
    scale = HEAD_SIZE ** (-0.5)
    factor = scale * math.log2(math.e)
    head = lax.axis_index("head")
    width = heads_at_once * HEAD_SIZE
    steps = group // heads_at_once

    def start_of(slot):
        return pl.multiple_of(slot * block + head * rows, rows)

    for slot in range(slots):
        key = start_of(slot) + lax.broadcasted_iota(jnp.int32, (length, rows), 0)
        own = start_of(slot) + WINDOW + lax.broadcasted_iota(jnp.int32, (length, rows), 1)
        bias[slot] = jnp.where((key >= low_ref[slot]) & (key <= own), 0.0, MASKED)

    def one_head(g, unused):
        acc[...] = jnp.zeros_like(acc)

        def one_step(step, unused):
            slot = step // steps
            first = pl.multiple_of(g * (group * HEAD_SIZE) + (step % steps) * width, width)
            keys_at = pl.ds(start_of(slot), length)
            keys, values = win[0, g, keys_at, :], win[1, g, keys_at, :]

            def stacked(ref):
                wide = ref[slot, :, pl.ds(first, width)]
                return jnp.concatenate(
                    [wide[:, n * HEAD_SIZE:(n + 1) * HEAD_SIZE] for n in range(heads_at_once)], axis=0
                )

            query, grad = stacked(q2), stacked(g2)
            nt = (((1,), (1,)), ((), ()))
            tn = (((0,), (0,)), ((), ()))
            f32 = jnp.float32
            scores = lax.dot_general(keys, query, nt, preferred_element_type=f32)
            shift = bias[slot]
            scores = scores * factor + jnp.concatenate([shift] * heads_at_once, axis=1)
            top = jnp.max(scores, axis=0, keepdims=True)
            probs = jnp.exp2(scores - top)
            total = jnp.sum(probs, axis=0, keepdims=True)
            probs = probs * (1.0 / total)
            weights = probs.astype(jnp.bfloat16)
            out = lax.dot_general(values, weights, tn, preferred_element_type=f32)
            out = out.astype(jnp.bfloat16).astype(f32)
            delta = jnp.sum(out * grad.astype(f32).T, axis=0, keepdims=True)
            prob_grad = lax.dot_general(values, grad, nt, preferred_element_type=f32)
            score_grad = (probs * (prob_grad - delta)).astype(jnp.bfloat16)
            dq = lax.dot_general(keys, score_grad, tn, preferred_element_type=f32) * scale
            acc[0, keys_at, :] += jnp.dot(score_grad, query, preferred_element_type=f32)
            acc[1, keys_at, :] += jnp.dot(weights, grad, preferred_element_type=f32)
            out_rows, dq_rows = out.T.astype(jnp.bfloat16), dq.T.astype(jnp.bfloat16)
            for n in range(heads_at_once):
                at = pl.ds(pl.multiple_of(first + n * HEAD_SIZE, HEAD_SIZE), HEAD_SIZE)
                out2[slot, :, at] = out_rows[n * rows:(n + 1) * rows]
                dq2[slot, :, at] = dq_rows[n * rows:(n + 1) * rows]
            return 0

        lax.fori_loop(0, slots * steps, one_step, 0)
        dkv[0, g] = (acc[0] * scale).astype(jnp.bfloat16)
        dkv[1, g] = acc[1].astype(jnp.bfloat16)
        return 0

    lax.fori_loop(0, kv_heads, one_head, 0)


def scatter_kernel(
    pairs, heads, back,
    out2, dq2, dkv,
    out, dq, result,
    passed, arrived, summed, far, total,
    local_sem, core_send, core_recv, far_send, far_recv, head_send, head_recv,
):
    ctx, head = lax.axis_index("ctx"), lax.axis_index("head")
    pair, core = ctx // 2, ctx % 2
    rows = out.shape[0]
    half = out.shape[1] // 2
    partner = pair * 2 + 1 - core
    keep = pl.ds(pl.multiple_of(core * half, half), half)
    f32 = jnp.float32

    def at(h):
        return pl.ds(pl.multiple_of(h * rows, rows), rows)

    greet(pairs, heads, back)

    def collect(k, d):
        to = lax.rem(head + d, heads)
        return remote(
            dkv.at[:, :, back - k, :, at(to), :], arrived.at[d - 1, k],
            head_send.at[d - 1, k], head_recv.at[d - 1, k], ctx, to,
        )

    def behind(k):
        return remote(summed.at[k], far.at[k - 1], far_send.at[k - 1], far_recv.at[k - 1], ctx - 2 * k, head)

    for k in range(back, -1, -1):

        @pl.when(pair - k >= 0)
        def _():
            for d in range(1, heads):
                collect(k, d).start()

    to_core = [
        remote(out2.at[1 - core], out.at[:, keep], core_send.at[0], core_recv.at[0], partner, head),
        remote(dq2.at[1 - core], dq.at[:, keep], core_send.at[1], core_recv.at[1], partner, head),
    ]
    on_chip = [
        pltpu.make_async_copy(out2.at[core], out.at[:, keep], local_sem.at[0]),
        pltpu.make_async_copy(dq2.at[core], dq.at[:, keep], local_sem.at[1]),
    ]
    for copy in to_core + on_chip:
        copy.start()
    for k in range(back, -1, -1):

        @pl.when(pair - k >= 0)
        def _():
            part = dkv[:, :, back - k, :, at(head), :].astype(f32)
            for d in range(1, heads):
                collect(k, d).wait_recv()
                part = part + arrived[d - 1, k].astype(f32)
            summed[k] = part.astype(jnp.bfloat16)
            if k > 0:
                behind(k).start()

    passed[...] = summed[0].astype(f32)
    for k in range(1, back + 1):

        @pl.when(pair + k < pairs)
        def _():
            behind(k).wait_recv()
            passed[...] = passed[...] + far[k - 1].astype(f32)

    total[...] = passed[...].astype(jnp.bfloat16)
    last = [
        remote(total.at[:, :, 1 - core], result.at[core], core_send.at[2], core_recv.at[2], partner, head),
        pltpu.make_async_copy(total.at[:, :, core], result.at[core], local_sem.at[2]),
    ]
    for copy in last:
        copy.start()
    for k in range(back, -1, -1):

        @pl.when(pair - k >= 0)
        def _():
            for d in range(1, heads):
                collect(k, d).wait_send()
            if k > 0:
                behind(k).wait_send()

    for copy in to_core + on_chip + last:
        copy.wait()


def local(pairs, heads, queries, key_heads, value_head_array, out_grad, doc_ids):
    rows, width = queries.shape
    kv_heads = key_heads.shape[1] // HEAD_SIZE
    half_kv = kv_heads // 2
    block = doc_ids.shape[0]
    back = -(-WINDOW // (2 * block))
    bf16, f32 = jnp.bfloat16, jnp.float32
    DMA = pltpu.SemaphoreType.DMA
    params = functools.partial(pltpu.CompilerParams, vmem_limit_bytes=60 * 1024 * 1024)

    kv = jnp.stack([key_heads, value_head_array]).reshape(2, rows, 2, half_kv, HEAD_SIZE)
    kv = jnp.transpose(kv, (2, 0, 3, 1, 4))
    docs_here = doc_ids.reshape(1, block)
    two = jax.ShapeDtypeStruct((2, rows, width // 2), bf16)
    window = jax.ShapeDtypeStruct((2, half_kv, back + 1, 2, block, HEAD_SIZE), bf16)
    q2, g2, win, docs = pl.pallas_call(
        functools.partial(gather_kernel, pairs, heads, back),
        out_shape=(two, two, window, jax.ShapeDtypeStruct((back + 1, 2, 1, block), jnp.int32)),
        in_specs=[VMEM] * 4,
        out_specs=(VMEM,) * 4,
        scratch_shapes=[
            DMA((4,)), DMA((4,)), DMA((4,)), DMA((back,)), DMA((back,)),
            DMA((heads - 1, back + 1)), DMA((heads - 1, back + 1)), DMA((back,)), DMA((back,)),
        ],
        compiler_params=params(collective_id=0, has_side_effects=True),
    )(queries, out_grad, kv, docs_here)

    span = (back + 1) * 2 * block
    doc_keys = docs.reshape(span)
    head = lax.axis_index("head")
    doc_rows = lax.dynamic_slice_in_dim(docs[back, :, 0, :], head * rows, rows, 1)
    at = jnp.arange(span, dtype=jnp.int32)
    own = WINDOW + (jnp.arange(2, dtype=jnp.int32) * block)[:, None] + head * rows + jnp.arange(rows, dtype=jnp.int32)
    earlier = (doc_rows[:, :, None] == doc_keys) & (at < own[:, :, None])
    first = own - jnp.sum(earlier.astype(jnp.int32), axis=-1)
    low = jnp.maximum(first, own - (WINDOW - 1)).reshape(2, 1, rows)

    length = WINDOW + rows
    out2, dq2, dkv = pl.pallas_call(
        functools.partial(attend_kernel, rows, 2),
        out_shape=(two, two, jax.ShapeDtypeStruct((2, half_kv, span, HEAD_SIZE), bf16)),
        in_specs=[VMEM] * 4,
        out_specs=(VMEM,) * 3,
        scratch_shapes=[pltpu.VMEM((2, length, rows), f32), pltpu.VMEM((2, span, HEAD_SIZE), f32)],
        compiler_params=params(),
    )(low, q2, g2, win.reshape(2, half_kv, span, HEAD_SIZE))

    piece = (2, half_kv, 2, rows, HEAD_SIZE)
    whole = jax.ShapeDtypeStruct((rows, width), bf16)
    out, dq, result = pl.pallas_call(
        functools.partial(scatter_kernel, pairs, heads, back),
        out_shape=(whole, whole, jax.ShapeDtypeStruct((2, 2, half_kv, rows, HEAD_SIZE), bf16)),
        in_specs=[VMEM] * 3,
        out_specs=(VMEM,) * 3,
        scratch_shapes=[
            pltpu.VMEM(piece, f32),
            pltpu.VMEM((heads - 1, back + 1) + piece, bf16),
            pltpu.VMEM((back + 1,) + piece, bf16),
            pltpu.VMEM((back,) + piece, bf16),
            pltpu.VMEM(piece, bf16),
            DMA((3,)), DMA((3,)), DMA((3,)), DMA((back,)), DMA((back,)),
            DMA((heads - 1, back + 1)), DMA((heads - 1, back + 1)),
        ],
        compiler_params=params(collective_id=1, has_side_effects=True),
    )(out2, dq2, dkv.reshape(window.shape))
    both = jnp.transpose(result, (1, 3, 0, 2, 4)).reshape(2, rows, kv_heads * HEAD_SIZE)
    return (out, dq, both[0], both[1])


def solution(mesh):
    tokens = P(("ctx", "head"), None)
    return jax.shard_map(
        functools.partial(local, mesh.shape["ctx"] // 2, mesh.shape["head"]),
        mesh=mesh,
        in_specs=(tokens, tokens, tokens, tokens, P("ctx")),
        out_specs=(tokens, tokens, tokens, tokens),
        check_vma=False,
    )
```

```python
import functools
import math

import jax
import jax.numpy as jnp
from jax import lax
from jax.experimental import pallas as pl
from jax.experimental.pallas import tpu as pltpu
from jax.sharding import PartitionSpec as P

HEAD_SIZE = 128
WINDOW = 1536
MASKED = -1e30
MESH = pl.DeviceIdType.MESH
VMEM = pl.BlockSpec(memory_space=pltpu.VMEM)


def remote(src, dst, send_sem, recv_sem, ctx, head):
    return pltpu.make_async_remote_copy(
        src_ref=src,
        dst_ref=dst,
        send_sem=send_sem,
        recv_sem=recv_sem,
        device_id={"ctx": ctx, "head": head},
        device_id_type=MESH,
    )


def greet(pairs, heads, back):
    ctx, head = lax.axis_index("ctx"), lax.axis_index("head")
    pair, core = ctx // 2, ctx % 2
    barrier = pltpu.get_barrier_semaphore()

    def signal(to_ctx, to_head):
        pl.semaphore_signal(
            barrier, inc=1, device_id={"ctx": to_ctx, "head": to_head}, device_id_type=MESH
        )

    signal(pair * 2 + 1 - core, head)
    for d in range(1, heads):
        signal(ctx, lax.rem(head + d, heads))
    for k in range(1, back + 1):
        for other in (pair + k, pair + pairs - k):
            signal(lax.rem(other, pairs) * 2 + core, head)
    pl.semaphore_wait(barrier, heads + 2 * back)


def fused_kernel(
    pairs, heads, back, heads_at_once,
    q_ref, g_ref, kv_ref, doc_ref,
    out, dq, result,
    q2, g2, win, docs, key_docs, bias, acc, out2, dq2, dkv, arrived, summed, far, total,
    local_sem, core_send, core_recv, doc_send, doc_recv,
    far_send, far_recv, head_send, head_recv,
    part_send, part_recv, back_send, back_recv, out_send, out_recv, out_local,
):
    ctx, head = lax.axis_index("ctx"), lax.axis_index("head")
    pair, core = ctx // 2, ctx % 2
    rows = q_ref.shape[0]
    half = q_ref.shape[1] // 2
    slots, block = 2, docs.shape[-1]
    kv_heads = win.shape[1]
    span = (back + 1) * slots * block
    group = half // HEAD_SIZE // kv_heads
    partner = pair * 2 + 1 - core
    length = WINDOW + rows
    scale = HEAD_SIZE ** (-0.5)
    factor = scale * math.log2(math.e)
    width = heads_at_once * HEAD_SIZE
    steps = group // heads_at_once
    f32, bf16 = jnp.float32, jnp.bfloat16
    flat = win.reshape(2, kv_heads, span, HEAD_SIZE)

    def at(h):
        return pl.ds(pl.multiple_of(h * rows, rows), rows)

    def columns(which, g=None):
        if g is None:
            return pl.ds(pl.multiple_of(which * half, half), half)
        size = group * HEAD_SIZE
        return pl.ds(pl.multiple_of(which * half + g * size, size), size)

    mine = at(head)

    def region(k, g):
        return win.at[:, g, back - k, :, mine, :]

    def ahead(k, g):
        return remote(region(0, g), region(k, g), far_send.at[k - 1, g], far_recv.at[k - 1, g], ctx + 2 * k, head)

    def ahead_docs(k):
        return remote(docs.at[back], docs.at[back - k], doc_send.at[k - 1], doc_recv.at[k - 1], ctx + 2 * k, head)

    def spread(k, d, g):
        return remote(
            region(k, g), region(k, g), head_send.at[d - 1, k, g], head_recv.at[d - 1, k, g],
            ctx, lax.rem(head + d, heads),
        )

    def collect(k, d, g):
        to = lax.rem(head + d, heads)
        return remote(
            dkv.at[:, g, back - k, :, at(to), :], arrived.at[d - 1, k, g],
            part_send.at[d - 1, k, g], part_recv.at[d - 1, k, g], ctx, to,
        )

    def behind(k, g):
        return remote(summed.at[k, g], far.at[k - 1, g], back_send.at[k - 1, g], back_recv.at[k - 1, g], ctx - 2 * k, head)

    def returned(g):
        copies = []
        for n, (src, dst) in enumerate(((out2, out), (dq2, dq))):
            to = dst.at[:, columns(core, g)]
            copies.append(remote(src.at[1 - core, :, columns(0, g)], to, out_send.at[n, g], out_recv.at[n, g], partner, head))
            copies.append(pltpu.make_async_copy(src.at[core, :, columns(0, g)], to, out_local.at[n, g]))
        return copies

    def each(make, lower, upper):
        for k in range(1, back + 1):
            if lower:
                pl.when(pair - k >= 0)(functools.partial(make, k))
            if upper:
                pl.when(pair + k < pairs)(functools.partial(make, k))

    greet(pairs, heads, back)
    to_core = [
        remote(doc_ref, docs.at[back, core], core_send.at[0], core_recv.at[0], partner, head),
        remote(kv_ref.at[1 - core], win.at[:, :, back, core, mine, :], core_send.at[1], core_recv.at[1], partner, head),
        remote(q_ref.at[:, columns(1 - core)], q2.at[core], core_send.at[2], core_recv.at[2], partner, head),
        remote(g_ref.at[:, columns(1 - core)], g2.at[core], core_send.at[3], core_recv.at[3], partner, head),
    ]
    on_chip = [
        pltpu.make_async_copy(doc_ref, docs.at[back, core], local_sem.at[0]),
        pltpu.make_async_copy(kv_ref.at[core], win.at[:, :, back, core, mine, :], local_sem.at[1]),
        pltpu.make_async_copy(q_ref.at[:, columns(core)], q2.at[core], local_sem.at[2]),
        pltpu.make_async_copy(g_ref.at[:, columns(core)], g2.at[core], local_sem.at[3]),
    ]
    for copy in to_core + on_chip:
        copy.start()
    for k in range(1, back + 1):

        @pl.when(pair - k < 0)
        def _():
            win[:, :, back - k] = jnp.zeros(win.shape[:2] + win.shape[3:], win.dtype)
            docs[back - k] = jnp.full(docs.shape[1:], -1, docs.dtype)

    for n in range(2):
        on_chip[n].wait()
        to_core[n].wait_recv()
    each(lambda k: ahead_docs(k).start(), False, True)

    def send_keys(g, unused):
        each(lambda k: ahead(k, g).start(), False, True)
        for d in range(1, heads):
            spread(0, d, g).start()
        return 0

    lax.fori_loop(0, kv_heads, send_keys, 0)

    def forward(g):
        def one(k):
            ahead(k, g).wait_recv()
            for d in range(1, heads):
                spread(k, d, g).start()

        each(one, True, False)

    def ready(g):
        for d in range(1, heads):
            spread(0, d, g).wait()

        def one(k):
            for d in range(1, heads):
                spread(k, d, g).wait()

        each(one, True, False)

    def reduce_parts(g):
        for k in range(back, -1, -1):

            @pl.when(pair - k >= 0)
            def _():
                part = dkv[:, g, back - k, :, mine, :].astype(f32)
                for d in range(1, heads):
                    collect(k, d, g).wait_recv()
                    part = part + arrived[d - 1, k, g].astype(f32)
                summed[k, g] = part.astype(bf16)
                if k > 0:
                    behind(k, g).start()

    def finish(g):
        acc_here = acc.at[:, pl.ds(0, slots * rows), :]
        acc_here[...] = summed[0, g].astype(f32).reshape(acc_here.shape)

        def one(k):
            behind(k, g).wait_recv()
            acc_here[...] = acc_here[...] + far[k - 1, g].astype(f32).reshape(acc_here.shape)

        each(one, False, True)
        total[:, g] = acc_here[...].astype(bf16).reshape(2, slots, rows, HEAD_SIZE)

    each(lambda k: ahead_docs(k).wait_recv(), True, False)
    tile = 128
    for k in range(back + 1):
        for slot in range(slots):
            for n in range(block // tile):
                row = docs[k, slot, :, n * tile:(n + 1) * tile].astype(f32)
                column = jnp.broadcast_to(row, (tile, tile)).T
                key_docs[pl.ds((k * slots + slot) * block + n * tile, tile), :] = column[:, :rows]

    def start_of(slot):
        return pl.multiple_of(slot * block + head * rows, rows)

    for slot in range(slots):
        query_doc = docs[back, slot, :, 0:rows]
        for h in range(1, heads):
            query_doc = jnp.where(head == h, docs[back, slot, :, h * rows:(h + 1) * rows], query_doc)
        apart = lax.broadcasted_iota(jnp.int32, (length, rows), 1) + WINDOW - lax.broadcasted_iota(jnp.int32, (length, rows), 0)
        same = key_docs[pl.ds(start_of(slot), length), :] == query_doc.astype(f32)
        bias[slot] = jnp.where(same & (apart >= 0) & (apart < WINDOW), 0.0, MASKED)

    forward(0)
    for n in range(2, 4):
        on_chip[n].wait()
        to_core[n].wait_recv()

    def one_head(g, unused):
        ready(g)

        @pl.when(g + 1 < kv_heads)
        def _():
            forward(g + 1)

        @pl.when(g >= 2)
        def _():
            finish(g - 2)

        acc[...] = jnp.zeros_like(acc)

        def one_slot(slot, unused):
            keys_at = pl.ds(start_of(slot), length)

            def one_step(step, unused):
                first = pl.multiple_of(g * (group * HEAD_SIZE) + step * width, width)
                keys, values = flat[0, g, keys_at, :], flat[1, g, keys_at, :]

                def stacked(ref):
                    wide = ref[slot, :, pl.ds(first, width)]
                    return jnp.concatenate(
                        [wide[:, n * HEAD_SIZE:(n + 1) * HEAD_SIZE] for n in range(heads_at_once)], axis=0
                    )

                query, grad = stacked(q2), stacked(g2)
                nt = (((1,), (1,)), ((), ()))
                tn = (((0,), (0,)), ((), ()))
                scores = lax.dot_general(keys, query, nt, preferred_element_type=f32)
                scores = scores * factor + jnp.concatenate([bias[slot]] * heads_at_once, axis=1)
                top = jnp.max(scores, axis=0, keepdims=True)
                probs = jnp.exp2(scores - top)
                probs = probs * (1.0 / jnp.sum(probs, axis=0, keepdims=True))
                weights = probs.astype(bf16)
                attended = lax.dot_general(values, weights, tn, preferred_element_type=f32)
                attended = attended.astype(bf16).astype(f32)
                delta = jnp.sum(attended * grad.astype(f32).T, axis=0, keepdims=True)
                prob_grad = lax.dot_general(values, grad, nt, preferred_element_type=f32)
                score_grad = (probs * (prob_grad - delta)).astype(bf16)
                query_grad = lax.dot_general(keys, score_grad, tn, preferred_element_type=f32) * scale
                acc[0, keys_at, :] += jnp.dot(score_grad, query, preferred_element_type=f32)
                acc[1, keys_at, :] += jnp.dot(weights, grad, preferred_element_type=f32)
                out_rows, dq_rows = attended.T.astype(bf16), query_grad.T.astype(bf16)
                for n in range(heads_at_once):
                    to = pl.ds(pl.multiple_of(first + n * HEAD_SIZE, HEAD_SIZE), HEAD_SIZE)
                    out2[slot, :, to] = out_rows[n * rows:(n + 1) * rows]
                    dq2[slot, :, to] = dq_rows[n * rows:(n + 1) * rows]
                return 0

            lax.fori_loop(0, steps, one_step, 0)

            @pl.when((slot == 0) & (g >= 1))
            def _():
                reduce_parts(g - 1)

            return 0

        lax.fori_loop(0, slots, one_slot, 0)
        dkv[0, g] = (acc[0] * scale).astype(bf16).reshape(dkv.shape[2:])
        dkv[1, g] = acc[1].astype(bf16).reshape(dkv.shape[2:])
        for k in range(back, -1, -1):

            @pl.when(pair - k >= 0)
            def _():
                for d in range(1, heads):
                    collect(k, d, g).start()

        for copy in returned(g):
            copy.start()
        return 0

    lax.fori_loop(0, kv_heads, one_head, 0)
    for g in range(max(kv_heads - 2, 0), kv_heads):
        if g == kv_heads - 1:
            reduce_parts(g)
        finish(g)
    last = [
        remote(total.at[:, :, 1 - core], result.at[core], core_send.at[4], core_recv.at[4], partner, head),
        pltpu.make_async_copy(total.at[:, :, core], result.at[core], local_sem.at[4]),
    ]
    for copy in last:
        copy.start()

    def drain(g, unused):
        for copy in returned(g):
            copy.wait()
        each(lambda k: ahead(k, g).wait_send(), False, True)
        for k in range(back + 1):

            @pl.when(pair - k >= 0)
            def _():
                for d in range(1, heads):
                    collect(k, d, g).wait_send()
                if k > 0:
                    behind(k, g).wait_send()

        return 0

    lax.fori_loop(0, kv_heads, drain, 0)
    each(lambda k: ahead_docs(k).wait_send(), False, True)
    for copy in to_core:
        copy.wait_send()
    for copy in last:
        copy.wait()


def local(pairs, heads, queries, key_heads, value_head_array, out_grad, doc_ids):
    rows, width = queries.shape
    kv_heads = key_heads.shape[1] // HEAD_SIZE
    half_kv = kv_heads // 2
    block = doc_ids.shape[0]
    back = -(-WINDOW // (2 * block))
    span = (back + 1) * 2 * block
    length = WINDOW + rows
    bf16, f32 = jnp.bfloat16, jnp.float32
    DMA = pltpu.SemaphoreType.DMA

    kv = jnp.stack([key_heads, value_head_array]).reshape(2, rows, 2, half_kv, HEAD_SIZE)
    kv = jnp.transpose(kv, (2, 0, 3, 1, 4))
    whole = jax.ShapeDtypeStruct((rows, width), bf16)
    two = pltpu.VMEM((2, rows, width // 2), bf16)
    window = pltpu.VMEM((2, half_kv, back + 1, 2, block, HEAD_SIZE), bf16)
    piece = (half_kv, 2, 2, rows, HEAD_SIZE)
    out, dq, result = pl.pallas_call(
        functools.partial(fused_kernel, pairs, heads, back, 2),
        out_shape=(whole, whole, jax.ShapeDtypeStruct((2, 2, half_kv, rows, HEAD_SIZE), bf16)),
        in_specs=[VMEM] * 4,
        out_specs=(VMEM,) * 3,
        scratch_shapes=[
            two, two, window,
            pltpu.VMEM((back + 1, 2, 1, block), jnp.int32),
            pltpu.VMEM((span, rows), f32),
            pltpu.VMEM((2, length, rows), f32),
            pltpu.VMEM((2, span, HEAD_SIZE), f32),
            two, two, window,
            pltpu.VMEM((heads - 1, back + 1) + piece, bf16),
            pltpu.VMEM((back + 1,) + piece, bf16),
            pltpu.VMEM((back,) + piece, bf16),
            pltpu.VMEM((2, half_kv, 2, rows, HEAD_SIZE), bf16),
            DMA((5,)), DMA((5,)), DMA((5,)), DMA((back,)), DMA((back,)),
            DMA((back, half_kv)), DMA((back, half_kv)),
            DMA((heads - 1, back + 1, half_kv)), DMA((heads - 1, back + 1, half_kv)),
            DMA((heads - 1, back + 1, half_kv)), DMA((heads - 1, back + 1, half_kv)),
            DMA((back, half_kv)), DMA((back, half_kv)),
            DMA((2, half_kv)), DMA((2, half_kv)), DMA((2, half_kv)),
        ],
        compiler_params=pltpu.CompilerParams(
            collective_id=0, has_side_effects=True, vmem_limit_bytes=63 * 1024 * 1024
        ),
    )(queries, out_grad, kv, doc_ids.reshape(1, block))
    both = jnp.transpose(result, (1, 3, 0, 2, 4)).reshape(2, rows, kv_heads * HEAD_SIZE)
    return (out, dq, both[0], both[1])


def solution(mesh):
    tokens = P(("ctx", "head"), None)
    return jax.shard_map(
        functools.partial(local, mesh.shape["ctx"] // 2, mesh.shape["head"]),
        mesh=mesh,
        in_specs=(tokens, tokens, tokens, tokens, P("ctx")),
        out_specs=(tokens, tokens, tokens, tokens),
        check_vma=False,
    )
```

```python
import functools
import math

import jax
import jax.numpy as jnp
from jax import lax
from jax.experimental import pallas as pl
from jax.experimental.pallas import tpu as pltpu
from jax.sharding import PartitionSpec as P

HEAD_SIZE = 128
WINDOW = 1536
MASKED = -1e30
MESH = pl.DeviceIdType.MESH
VMEM = pl.BlockSpec(memory_space=pltpu.VMEM)


def remote(src, dst, send_sem, recv_sem, ctx, head):
    return pltpu.make_async_remote_copy(
        src_ref=src,
        dst_ref=dst,
        send_sem=send_sem,
        recv_sem=recv_sem,
        device_id={"ctx": ctx, "head": head},
        device_id_type=MESH,
    )


def greet(pairs, heads, back):
    ctx, head = lax.axis_index("ctx"), lax.axis_index("head")
    pair, core = ctx // 2, ctx % 2
    barrier = pltpu.get_barrier_semaphore()

    def signal(to_ctx, to_head):
        pl.semaphore_signal(
            barrier, inc=1, device_id={"ctx": to_ctx, "head": to_head}, device_id_type=MESH
        )

    signal(pair * 2 + 1 - core, head)
    for d in range(1, heads):
        signal(ctx, lax.rem(head + d, heads))
    for k in range(1, back + 1):
        for other in (pair + k, pair + pairs - k):
            signal(lax.rem(other, pairs) * 2 + core, head)
    pl.semaphore_wait(barrier, heads + 2 * back)


def fused_kernel(
    pairs, heads, back, heads_at_once,
    q_ref, g_ref, kv_ref, doc_ref,
    out, dq, result,
    q2, g2, win, docs, key_docs, bias, acc, out2, dq2, dkv, arrived, summed, far, total,
    local_sem, core_send, core_recv, doc_send, doc_recv,
    far_send, far_recv, head_send, head_recv,
    part_send, part_recv, back_send, back_recv, out_send, out_recv, out_local,
):
    ctx, head = lax.axis_index("ctx"), lax.axis_index("head")
    pair, core = ctx // 2, ctx % 2
    rows = q_ref.shape[0]
    half = q_ref.shape[1] // 2
    slots, block = 2, docs.shape[-1]
    kv_heads = win.shape[1]
    span = (back + 1) * slots * block
    group = half // HEAD_SIZE // kv_heads
    partner = pair * 2 + 1 - core
    length = WINDOW + rows
    scale = HEAD_SIZE ** (-0.5)
    factor = scale * math.log2(math.e)
    width = heads_at_once * HEAD_SIZE
    steps = group // heads_at_once
    f32, bf16 = jnp.float32, jnp.bfloat16
    flat = win.reshape(2, kv_heads, span, HEAD_SIZE)

    def at(h):
        return pl.ds(pl.multiple_of(h * rows, rows), rows)

    def columns(which, g=None):
        if g is None:
            return pl.ds(pl.multiple_of(which * half, half), half)
        size = group * HEAD_SIZE
        return pl.ds(pl.multiple_of(which * half + g * size, size), size)

    mine = at(head)

    def region(k, g):
        return win.at[:, g, back - k, :, mine, :]

    def ahead(k, g):
        return remote(region(0, g), region(k, g), far_send.at[k - 1, g], far_recv.at[k - 1, g], ctx + 2 * k, head)

    def ahead_docs(k):
        return remote(docs.at[back], docs.at[back - k], doc_send.at[k - 1], doc_recv.at[k - 1], ctx + 2 * k, head)

    def spread(k, d, g):
        return remote(
            region(k, g), region(k, g), head_send.at[d - 1, k, g], head_recv.at[d - 1, k, g],
            ctx, lax.rem(head + d, heads),
        )

    def collect(k, d, g):
        to = lax.rem(head + d, heads)
        return remote(
            dkv.at[:, g, back - k, :, at(to), :], arrived.at[d - 1, k, g],
            part_send.at[d - 1, k, g], part_recv.at[d - 1, k, g], ctx, to,
        )

    def behind(k, g):
        return remote(summed.at[k, g], far.at[k - 1, g], back_send.at[k - 1, g], back_recv.at[k - 1, g], ctx - 2 * k, head)

    def returned(g):
        copies = []
        for n, (src, dst) in enumerate(((out2, out), (dq2, dq))):
            to = dst.at[:, columns(core, g)]
            copies.append(remote(src.at[1 - core, :, columns(0, g)], to, out_send.at[n, g], out_recv.at[n, g], partner, head))
            copies.append(pltpu.make_async_copy(src.at[core, :, columns(0, g)], to, out_local.at[n, g]))
        return copies

    def each(make, lower, upper):
        for k in range(1, back + 1):
            if lower:
                pl.when(pair - k >= 0)(functools.partial(make, k))
            if upper:
                pl.when(pair + k < pairs)(functools.partial(make, k))

    greet(pairs, heads, back)
    to_core = [
        remote(doc_ref, docs.at[back, core], core_send.at[0], core_recv.at[0], partner, head),
        remote(kv_ref.at[1 - core], win.at[:, :, back, core, mine, :], core_send.at[1], core_recv.at[1], partner, head),
        remote(q_ref.at[:, columns(1 - core)], q2.at[core], core_send.at[2], core_recv.at[2], partner, head),
        remote(g_ref.at[:, columns(1 - core)], g2.at[core], core_send.at[3], core_recv.at[3], partner, head),
    ]
    on_chip = [
        pltpu.make_async_copy(doc_ref, docs.at[back, core], local_sem.at[0]),
        pltpu.make_async_copy(kv_ref.at[core], win.at[:, :, back, core, mine, :], local_sem.at[1]),
        pltpu.make_async_copy(q_ref.at[:, columns(core)], q2.at[core], local_sem.at[2]),
        pltpu.make_async_copy(g_ref.at[:, columns(core)], g2.at[core], local_sem.at[3]),
    ]
    for copy in to_core + on_chip:
        copy.start()
    for k in range(1, back + 1):

        @pl.when(pair - k < 0)
        def _():
            win[:, :, back - k] = jnp.zeros(win.shape[:2] + win.shape[3:], win.dtype)
            docs[back - k] = jnp.full(docs.shape[1:], -1, docs.dtype)

    for n in range(2):
        on_chip[n].wait()
        to_core[n].wait_recv()
    each(lambda k: ahead_docs(k).start(), False, True)

    def send_keys(g, unused):
        each(lambda k: ahead(k, g).start(), False, True)
        for d in range(1, heads):
            spread(0, d, g).start()
        return 0

    lax.fori_loop(0, kv_heads, send_keys, 0)

    def forward(g):
        def one(k):
            ahead(k, g).wait_recv()
            for d in range(1, heads):
                spread(k, d, g).start()

        each(one, True, False)

    def ready(g):
        for d in range(1, heads):
            spread(0, d, g).wait()

        def one(k):
            for d in range(1, heads):
                spread(k, d, g).wait()

        each(one, True, False)

    def reduce_parts(g):
        for k in range(back, -1, -1):

            @pl.when(pair - k >= 0)
            def _():
                part = dkv[:, g, back - k, :, mine, :].astype(f32)
                for d in range(1, heads):
                    collect(k, d, g).wait_recv()
                    part = part + arrived[d - 1, k, g].astype(f32)
                summed[k, g] = part.astype(bf16)
                if k > 0:
                    behind(k, g).start()

    def finish(g):
        acc_here = acc.at[:, pl.ds(0, slots * rows), :]
        acc_here[...] = summed[0, g].astype(f32).reshape(acc_here.shape)

        def one(k):
            behind(k, g).wait_recv()
            acc_here[...] = acc_here[...] + far[k - 1, g].astype(f32).reshape(acc_here.shape)

        each(one, False, True)
        total[:, g] = acc_here[...].astype(bf16).reshape(2, slots, rows, HEAD_SIZE)

    each(lambda k: ahead_docs(k).wait_recv(), True, False)
    tile = 128
    for k in range(back + 1):
        for slot in range(slots):
            for n in range(block // tile):
                row = docs[k, slot, :, n * tile:(n + 1) * tile].astype(f32)
                column = jnp.broadcast_to(row, (tile, tile)).T
                key_docs[pl.ds((k * slots + slot) * block + n * tile, tile), :] = column[:, :rows]

    def start_of(slot):
        return pl.multiple_of(slot * block + head * rows, rows)

    for slot in range(slots):
        query_doc = docs[back, slot, :, 0:rows]
        for h in range(1, heads):
            query_doc = jnp.where(head == h, docs[back, slot, :, h * rows:(h + 1) * rows], query_doc)
        apart = lax.broadcasted_iota(jnp.int32, (length, rows), 1) + WINDOW - lax.broadcasted_iota(jnp.int32, (length, rows), 0)
        same = key_docs[pl.ds(start_of(slot), length), :] == query_doc.astype(f32)
        bias[slot] = jnp.where(same & (apart >= 0) & (apart < WINDOW), 0.0, MASKED)

    forward(0)
    for n in range(2, 4):
        on_chip[n].wait()
        to_core[n].wait_recv()

    def one_head(g, unused):
        ready(g)

        @pl.when(g + 1 < kv_heads)
        def _():
            forward(g + 1)

        @pl.when(g >= 2)
        def _():
            finish(g - 2)

        acc[...] = jnp.zeros_like(acc)

        def one_slot(slot, unused):
            keys_at = pl.ds(start_of(slot), length)

            def one_step(step, unused):
                first = pl.multiple_of(g * (group * HEAD_SIZE) + step * width, width)
                keys, values = flat[0, g, keys_at, :], flat[1, g, keys_at, :]

                def stacked(ref):
                    wide = ref[slot, :, pl.ds(first, width)]
                    return jnp.concatenate(
                        [wide[:, n * HEAD_SIZE:(n + 1) * HEAD_SIZE] for n in range(heads_at_once)], axis=0
                    )

                query, grad = stacked(q2), stacked(g2)
                nt = (((1,), (1,)), ((), ()))
                tn = (((0,), (0,)), ((), ()))
                scores = lax.dot_general(keys, query, nt, preferred_element_type=f32)
                scores = scores * factor + jnp.concatenate([bias[slot]] * heads_at_once, axis=1)
                top = jnp.max(scores, axis=0, keepdims=True)
                probs = jnp.exp2(scores - top)
                inverse = 1.0 / jnp.sum(probs, axis=0, keepdims=True)
                by_row = jnp.broadcast_to(inverse, (HEAD_SIZE, inverse.shape[1])).T
                weights = probs.astype(bf16)
                attended = lax.dot_general(values, weights, tn, preferred_element_type=f32)
                attended = (attended * inverse).astype(bf16).astype(f32)
                delta = jnp.sum(attended * grad.astype(f32).T, axis=0, keepdims=True)
                prob_grad = lax.dot_general(values, grad, nt, preferred_element_type=f32)
                score_grad = (probs * (prob_grad - delta)).astype(bf16)
                query_grad = lax.dot_general(keys, score_grad, tn, preferred_element_type=f32) * (scale * inverse)
                acc[0, keys_at, :] += jnp.dot(score_grad, (query.astype(f32) * by_row).astype(bf16), preferred_element_type=f32)
                acc[1, keys_at, :] += jnp.dot(weights, (grad.astype(f32) * by_row).astype(bf16), preferred_element_type=f32)
                out_rows, dq_rows = attended.T.astype(bf16), query_grad.T.astype(bf16)
                for n in range(heads_at_once):
                    to = pl.ds(pl.multiple_of(first + n * HEAD_SIZE, HEAD_SIZE), HEAD_SIZE)
                    out2[slot, :, to] = out_rows[n * rows:(n + 1) * rows]
                    dq2[slot, :, to] = dq_rows[n * rows:(n + 1) * rows]
                return 0

            lax.fori_loop(0, steps, one_step, 0)

            @pl.when((slot == 0) & (g >= 1))
            def _():
                reduce_parts(g - 1)

            return 0

        lax.fori_loop(0, slots, one_slot, 0)
        dkv[0, g] = (acc[0] * scale).astype(bf16).reshape(dkv.shape[2:])
        dkv[1, g] = acc[1].astype(bf16).reshape(dkv.shape[2:])
        for k in range(back, -1, -1):

            @pl.when(pair - k >= 0)
            def _():
                for d in range(1, heads):
                    collect(k, d, g).start()

        for copy in returned(g):
            copy.start()
        return 0

    lax.fori_loop(0, kv_heads, one_head, 0)
    for g in range(max(kv_heads - 2, 0), kv_heads):
        if g == kv_heads - 1:
            reduce_parts(g)
        finish(g)
    last = [
        remote(total.at[:, :, 1 - core], result.at[core], core_send.at[4], core_recv.at[4], partner, head),
        pltpu.make_async_copy(total.at[:, :, core], result.at[core], local_sem.at[4]),
    ]
    for copy in last:
        copy.start()

    def drain(g, unused):
        for copy in returned(g):
            copy.wait()
        each(lambda k: ahead(k, g).wait_send(), False, True)
        for k in range(back + 1):

            @pl.when(pair - k >= 0)
            def _():
                for d in range(1, heads):
                    collect(k, d, g).wait_send()
                if k > 0:
                    behind(k, g).wait_send()

        return 0

    lax.fori_loop(0, kv_heads, drain, 0)
    each(lambda k: ahead_docs(k).wait_send(), False, True)
    for copy in to_core:
        copy.wait_send()
    for copy in last:
        copy.wait()


def local(pairs, heads, queries, key_heads, value_head_array, out_grad, doc_ids):
    rows, width = queries.shape
    kv_heads = key_heads.shape[1] // HEAD_SIZE
    half_kv = kv_heads // 2
    block = doc_ids.shape[0]
    back = -(-WINDOW // (2 * block))
    span = (back + 1) * 2 * block
    length = WINDOW + rows
    bf16, f32 = jnp.bfloat16, jnp.float32
    DMA = pltpu.SemaphoreType.DMA

    kv = jnp.stack([key_heads, value_head_array]).reshape(2, rows, 2, half_kv, HEAD_SIZE)
    kv = jnp.transpose(kv, (2, 0, 3, 1, 4))
    whole = jax.ShapeDtypeStruct((rows, width), bf16)
    two = pltpu.VMEM((2, rows, width // 2), bf16)
    window = pltpu.VMEM((2, half_kv, back + 1, 2, block, HEAD_SIZE), bf16)
    piece = (half_kv, 2, 2, rows, HEAD_SIZE)
    out, dq, result = pl.pallas_call(
        functools.partial(fused_kernel, pairs, heads, back, 8),
        out_shape=(whole, whole, jax.ShapeDtypeStruct((2, 2, half_kv, rows, HEAD_SIZE), bf16)),
        in_specs=[VMEM] * 4,
        out_specs=(VMEM,) * 3,
        scratch_shapes=[
            two, two, window,
            pltpu.VMEM((back + 1, 2, 1, block), jnp.int32),
            pltpu.VMEM((span, rows), f32),
            pltpu.VMEM((2, length, rows), f32),
            pltpu.VMEM((2, span, HEAD_SIZE), f32),
            two, two, window,
            pltpu.VMEM((heads - 1, back + 1) + piece, bf16),
            pltpu.VMEM((back + 1,) + piece, bf16),
            pltpu.VMEM((back,) + piece, bf16),
            pltpu.VMEM((2, half_kv, 2, rows, HEAD_SIZE), bf16),
            DMA((5,)), DMA((5,)), DMA((5,)), DMA((back,)), DMA((back,)),
            DMA((back, half_kv)), DMA((back, half_kv)),
            DMA((heads - 1, back + 1, half_kv)), DMA((heads - 1, back + 1, half_kv)),
            DMA((heads - 1, back + 1, half_kv)), DMA((heads - 1, back + 1, half_kv)),
            DMA((back, half_kv)), DMA((back, half_kv)),
            DMA((2, half_kv)), DMA((2, half_kv)), DMA((2, half_kv)),
        ],
        compiler_params=pltpu.CompilerParams(
            collective_id=0, has_side_effects=True, vmem_limit_bytes=63 * 1024 * 1024
        ),
    )(queries, out_grad, kv, doc_ids.reshape(1, block))
    both = jnp.transpose(result, (1, 3, 0, 2, 4)).reshape(2, rows, kv_heads * HEAD_SIZE)
    return (out, dq, both[0], both[1])


def solution(mesh):
    tokens = P(("ctx", "head"), None)
    return jax.shard_map(
        functools.partial(local, mesh.shape["ctx"] // 2, mesh.shape["head"]),
        mesh=mesh,
        in_specs=(tokens, tokens, tokens, tokens, P("ctx")),
        out_specs=(tokens, tokens, tokens, tokens),
        check_vma=False,
    )
```
